32 devices in a mesh: seq: 8 (over z, x), wa: 4 (over y, core).
Axes of the slice: x: 2, y: 2, z: 4, core: 2. Of those that a mesh axis runs over, the one named last changes fastest.
Arguments:
- tokens: bfloat16 [2048, 1024], P('seq'), may hold values from -6 to 6
- gain_mix: float32 [1024], replicated, may hold values from 0.5 to 1.5
- w_z: bfloat16 [1024, 1536], P('seq', 'wa'), may hold values from -0.1875 to 0.1875
- w_x: bfloat16 [1024, 1536], P('seq', 'wa'), may hold values from -0.1875 to 0.1875
- w_bc: bfloat16 [1024, 256], P('seq'), may hold values from -0.046875 to 0.046875
- w_dt: bfloat16 [1024, 24], P('seq', 'wa'), may hold values from -0.1875 to 0.1875
- conv_x: float32 [4, 1536], P(None, 'wa'), may hold values from -3 to 3
- conv_bc: float32 [4, 256], replicated, may hold values from -3 to 3
- dt_bias: float32 [24], P('wa'), may hold values from -1 to 1
- a_log: float32 [24], P('wa'), may hold values from -10.5 to -3
- d_skip: float32 [24], P('wa'), may hold values from 0.5 to 1.5
- w_out: bfloat16 [1536, 1024], P('wa', 'seq'), may hold values from -0.0390625 to 0.0390625
- w_q: bfloat16 [1024, 512], P('seq', 'wa'), may hold values from -0.1875 to 0.1875
- w_kv: bfloat16 [1024, 256], P('seq'), may hold values from -0.1875 to 0.1875
- w_o: bfloat16 [512, 1024], P('wa', 'seq'), may hold values from -1 to 1
- gain_ffn: float32 [1024], replicated, may hold values from 0.5 to 1.5
- w_gate: bfloat16 [1024, 2048], P('seq', 'wa'), may hold values from -0.1875 to 0.1875
- w_up: bfloat16 [1024, 2048], P('seq', 'wa'), may hold values from -0.1875 to 0.1875
- w_down: bfloat16 [2048, 1024], P('wa', 'seq'), may hold values from -0.125 to 0.125
- cotangent: bfloat16 [2048, 1024], P('seq'), may hold values from -6 to 6
Outputs:
- output: bfloat16 [2048, 1024], P('seq', 'wa')
- grad_tokens: float32 [2048, 1024], P('seq')
- grad_gain_mix: float32 [1024], replicated
- grad_w_z: float32 [1024, 1536], P('seq', 'wa')
- grad_w_x: float32 [1024, 1536], P('seq', 'wa')
- grad_w_bc: float32 [1024, 256], P('seq')
- grad_w_dt: float32 [1024, 24], P('seq', 'wa')
- grad_conv_x: float32 [4, 1536], P(None, 'wa')
- grad_conv_bc: float32 [4, 256], replicated
- grad_dt_bias: float32 [24], P('wa')
- grad_a_log: float32 [24], P('wa')
- grad_d_skip: float32 [24], P('wa')
- grad_w_out: float32 [1536, 1024], P('wa', 'seq')
- grad_w_q: float32 [1024, 512], P('seq', 'wa')
- grad_w_kv: float32 [1024, 256], P('seq')
- grad_w_o: float32 [512, 1024], P('wa', 'seq')
- grad_gain_ffn: float32 [1024], replicated
- grad_w_gate: float32 [1024, 2048], P('seq', 'wa')
- grad_w_up: float32 [1024, 2048], P('seq', 'wa')
- grad_w_down: float32 [2048, 1024], P('wa', 'seq')
The draws below stay inside these ranges and needn't reach their ends.
All inputs are finite; a program needn't handle non-finite values.
Results may differ from the reference program's by a relative error of at most 0.012.
Values may be sent and summed in bfloat16 or wider, within the bound.
A program may use at most 128 MiB of HBM per device.

```python
import jax
import jax.numpy as jnp
from jax import lax

D = 1024
MH = 24
SH = 64
NS = 128
CONVK = 4
QH = 8
KVH = 2
HD = 64
FF = 2048
TOK_DEV = 256
DI = 1536
TOKENS = 2048


def draw_a_log(key, part):
    slow_key = jax.random.fold_in(key, 31)
    fast_key = jax.random.fold_in(key, 32)
    order_key = jax.random.fold_in(key, 33)
    slow_rates = jax.random.uniform(slow_key, (MH,), jnp.float32, -10.5, -8.7)
    fast_rates = jax.random.uniform(fast_key, (MH,), jnp.float32, -5.5, -3.0)
    ranking = jax.random.permutation(order_key, MH)
    slow_count = MH // 2
    return jnp.where(ranking < slow_count, slow_rates, fast_rates).astype(jnp.float32)


def shard_levels(key, shape, shards, smallest, high):
    factor_of = 1.0
    for position, blocks in shards:
        heights = jax.random.uniform(jax.random.fold_in(jax.random.fold_in(key, 6), position), (blocks,), jnp.float32, smallest / len(shards), high / len(shards))
        factor_of = factor_of * jnp.repeat(jnp.exp(heights), shape[position] // blocks).reshape((-1,) + (1,) * (len(shape) - 1 - position))
    return factor_of


def bell_draw(stream_key, extent, scale, bound, split=(), held_as=jnp.bfloat16):
    factor_of = shard_levels(stream_key, extent, split, -0.22, 0.18) if split else 1.0
    values = jax.random.normal(stream_key, extent, jnp.float32) * scale * factor_of
    return jnp.minimum(jnp.maximum(values, -bound), bound).astype(held_as)


def setup_inputs(seed: int = 0) -> dict:
    seeds = jax.random.split(jax.random.key(seed), 21)
    return {
        "tokens": bell_draw(seeds[0], (TOKENS, D), 1.0, 6.0, ((0, 8),)),
        "gain_mix": jnp.clip(1.0 + 0.1 * jax.random.normal(seeds[1], (D,), jnp.float32), 0.5, 1.5),
        "w_z": bell_draw(seeds[2], (D, DI), D ** -0.5, 0.1875, ((0, 8), (1, 4))),
        "w_x": bell_draw(seeds[3], (D, DI), D ** -0.5, 0.1875, ((0, 8), (1, 4))),
        "w_bc": bell_draw(seeds[4], (D, 2 * NS), (16 * D) ** -0.5, 0.046875, ((0, 8),)),
        "w_dt": bell_draw(seeds[5], (D, MH), D ** -0.5, 0.1875, ((0, 8), (1, 4))),
        "conv_x": bell_draw(seeds[6], (CONVK, DI), CONVK ** -0.5, 3.0, ((1, 4),), jnp.float32),
        "conv_bc": bell_draw(seeds[7], (CONVK, 2 * NS), CONVK ** -0.5, 3.0, (), jnp.float32),
        "dt_bias": jnp.clip(jax.random.uniform(seeds[8], (MH,), jnp.float32, -1.0, 1.0) * shard_levels(seeds[8], (MH,), ((0, 4),), -0.4, 0.0), -1.0, 1.0),
        "a_log": draw_a_log(jax.random.fold_in(seeds[20], 71), 0),
        "d_skip": jnp.clip(0.5 + 1.0 * jax.random.uniform(seeds[10], (MH,), jnp.float32) ** shard_levels(seeds[10], (MH,), ((0, 4),), -0.2, 0.2), 0.5, 1.5),
        "w_out": bell_draw(seeds[11], (DI, D), (16 * DI) ** -0.5, 0.0390625, ((0, 4), (1, 8))),
        "w_q": bell_draw(seeds[12], (D, QH * HD), D ** -0.5, 0.1875, ((0, 8), (1, 4))),
        "w_kv": bell_draw(seeds[13], (D, 2 * KVH * HD), D ** -0.5, 0.1875, ((0, 8),)),
        "w_o": bell_draw(seeds[14], (QH * HD, D), (QH * HD // 16) ** -0.5, 1.0, ((0, 4), (1, 8))),
        "gain_ffn": jnp.clip(1.0 + 0.1 * jax.random.normal(seeds[15], (D,), jnp.float32), 0.5, 1.5),
        "w_gate": bell_draw(seeds[16], (D, FF), D ** -0.5, 0.1875, ((0, 8), (1, 4))),
        "w_up": bell_draw(seeds[17], (D, FF), D ** -0.5, 0.1875, ((0, 8), (1, 4))),
        "w_down": bell_draw(seeds[18], (FF, D), FF ** -0.5, 0.125, ((0, 4), (1, 8))),
        "cotangent": bell_draw(seeds[19], (TOKENS, D), 1.0, 6.0, ((0, 8),)),
    }


EPS = 1e-05
ROPE_BASE = 100000000000.0
highest = lax.Precision.HIGHEST

def bf16_keep(values):
    return lax.optimization_barrier(values.astype(jnp.bfloat16))

def project(left_side, right_side):
    return jnp.dot(left_side, right_side, preferred_element_type=jnp.float32)

def rms_scale(row_values):
    return lax.rsqrt(lax.optimization_barrier(jnp.mean(row_values * row_values, axis=-1, keepdims=True)) + EPS)

def rope_tables(positions):
    frequency = ROPE_BASE ** (-(jnp.arange(HD // 2, dtype=jnp.float32) * 2.0 / HD))
    angles = positions.astype(jnp.float32)[:, None] * frequency[None, :]
    return (jnp.cos(angles), jnp.sin(angles))

def rotate(values, cosine, sine):
    half_width = values.shape[-1] // 2
    first_half = values[..., :half_width]
    second_half = values[..., half_width:]
    cos_part = cosine[:, None, :]
    sin_part = sine[:, None, :]
    return jnp.concatenate([first_half * cos_part - second_half * sin_part, second_half * cos_part + first_half * sin_part], axis=-1)

def unrotate(gradients, cosine, sine):
    half_width = gradients.shape[-1] // 2
    first_half = gradients[..., :half_width]
    second_half = gradients[..., half_width:]
    cos_part = cosine[:, None, :]
    sin_part = sine[:, None, :]
    return jnp.concatenate([first_half * cos_part + second_half * sin_part, second_half * cos_part - first_half * sin_part], axis=-1)

def conv_silu(pre_values, kernel, edge_rows):
    length = pre_values.shape[0]
    padded = jnp.concatenate([edge_rows, pre_values], axis=0)
    running = kernel[0] * padded[0:length]
    for offset in range(1, CONVK):
        running = running + kernel[offset] * padded[offset:offset + length]
    return jax.nn.silu(running)

def prepare(x_input, bc_input, dt_input, edge_x, edge_bc, conv_x, conv_bc, dt_bias, a_log):
    length = x_input.shape[0]
    head_count = a_log.shape[0]
    x_conv = conv_silu(x_input, conv_x, edge_x).reshape(length, head_count, -1)
    bc_conv = conv_silu(bc_input, conv_bc, edge_bc)
    step_size = jax.nn.softplus(dt_input + dt_bias[None, :])
    log_decay = -jnp.exp(a_log)[None, :] * step_size
    return (x_conv, bc_conv[:, :NS], bc_conv[:, NS:], step_size, log_decay)

def ssd_state(x_conv, b_mat, step_size, log_decay):
    cumulative = jnp.cumsum(log_decay, axis=0)
    tail_weight = jnp.exp(cumulative[-1][None, :] - cumulative) * step_size
    local_state = jnp.einsum('sh,shp,sn->hpn', tail_weight, x_conv, b_mat, precision=highest)
    return (jnp.exp(cumulative[-1]), local_state)

def ssd_output(x_conv, b_mat, c_mat, step_size, log_decay, start_state):
    cumulative = jnp.cumsum(log_decay, axis=0)
    length = x_conv.shape[0]
    causal = jnp.arange(length, dtype=jnp.int32)[:, None] >= jnp.arange(length, dtype=jnp.int32)[None, :]
    gap_sums = cumulative[:, None, :] - cumulative[None, :, :]
    decays = jnp.exp(jnp.where(causal[:, :, None], gap_sums, -1e+30))
    intersections = jnp.dot(c_mat, b_mat.T, precision=highest)
    mixing = decays * intersections[:, :, None] * step_size[None, :, :]
    inner_part = jnp.einsum('tsh,shp->thp', mixing, x_conv, precision=highest)
    carried = jnp.einsum('tn,hpn->thp', c_mat, start_state, precision=highest) * jnp.exp(cumulative)[:, :, None]
    return inner_part + carried

def mixer_reference(z_proj, x_proj, bc_proj, dt_proj, conv_x, conv_bc, dt_bias, a_log, d_skip):
    edge_x = jnp.zeros((CONVK - 1, x_proj.shape[1]), jnp.float32)
    edge_bc = jnp.zeros((CONVK - 1, bc_proj.shape[1]), jnp.float32)
    x_conv, b_mat, c_mat, step_size, log_decay = prepare(x_proj, bc_proj, dt_proj, edge_x, edge_bc, conv_x, conv_bc, dt_bias, a_log)
    blocks = TOKENS // TOK_DEV

    def advance(state_now, pieces):
        x_block, b_block, c_block, step_block, decay_block = pieces
        outputs = ssd_output(x_block, b_block, c_block, step_block, decay_block, state_now)
        decay_total, local_state = ssd_state(x_block, b_block, step_block, decay_block)
        return (decay_total[:, None, None] * state_now + local_state, outputs)
    stacked = (x_conv.reshape(blocks, TOK_DEV, MH, SH), b_mat.reshape(blocks, TOK_DEV, NS), c_mat.reshape(blocks, TOK_DEV, NS), step_size.reshape(blocks, TOK_DEV, MH), log_decay.reshape(blocks, TOK_DEV, MH))
    _, outputs = lax.scan(advance, jnp.zeros((MH, SH, NS), jnp.float32), stacked)
    ssm_out = outputs.reshape(TOKENS, MH, SH) + d_skip[None, :, None] * x_conv
    return ssm_out.reshape(TOKENS, DI) * jax.nn.silu(z_proj)

def attention_forward(q_rot, k_rot, v_val):
    group_size = QH // KVH
    key_rows = jnp.repeat(k_rot, group_size, axis=1).astype(jnp.float32)
    value_rows = jnp.repeat(v_val, group_size, axis=1).astype(jnp.float32)
    block_size = 512 if TOKENS % 512 == 0 else TOKENS
    inv_root = HD ** (-0.5)
    key_pos = jnp.arange(TOKENS, dtype=jnp.int32)

    def one_block(start_row):
        queries = lax.dynamic_slice_in_dim(q_rot, start_row, block_size, 0).astype(jnp.float32)
        query_pos = start_row + jnp.arange(block_size, dtype=jnp.int32)
        scores = jnp.einsum('tgd,ngd->gtn', queries, key_rows) * inv_root
        allowed = key_pos[None, None, :] <= query_pos[None, :, None]
        row_max = lax.optimization_barrier(jnp.max(jnp.where(allowed, scores, -1e+30), axis=-1))
        weights = jnp.where(allowed, jnp.exp(scores - row_max[:, :, None]), 0.0)
        row_sum = lax.optimization_barrier(jnp.sum(weights, axis=-1))
        rounded = bf16_keep(weights).astype(jnp.float32)
        weighted_sum = jnp.einsum('gtn,ngd->tgd', rounded, value_rows)
        attn_block = bf16_keep(weighted_sum / row_sum.T[:, :, None])
        return (attn_block, (row_max + jnp.log(row_sum)).T)
    starts = jnp.arange(TOKENS // block_size, dtype=jnp.int32) * block_size
    attn_heads, log_sums = lax.map(one_block, starts)
    return (attn_heads.reshape(TOKENS, QH, HD), log_sums.reshape(TOKENS, QH))

def attention_backward(q_rot, k_rot, v_val, d_attn, log_sums, out_delta):
    group_size = QH // KVH
    key_rows = jnp.repeat(k_rot, group_size, axis=1).astype(jnp.float32)
    value_rows = jnp.repeat(v_val, group_size, axis=1).astype(jnp.float32)
    block_size = 512 if TOKENS % 512 == 0 else TOKENS
    inv_root = HD ** (-0.5)
    key_pos = jnp.arange(TOKENS, dtype=jnp.int32)

    def visit_block(totals, start_row):
        key_total, value_total = totals
        queries = lax.dynamic_slice_in_dim(q_rot, start_row, block_size, 0).astype(jnp.float32)
        grads_in = lax.dynamic_slice_in_dim(d_attn, start_row, block_size, 0).astype(jnp.float32)
        sums_in = lax.dynamic_slice_in_dim(log_sums, start_row, block_size, 0)
        delta_in = lax.dynamic_slice_in_dim(out_delta, start_row, block_size, 0)
        query_pos = start_row + jnp.arange(block_size, dtype=jnp.int32)
        scores = jnp.einsum('tgd,ngd->gtn', queries, key_rows) * inv_root
        allowed = key_pos[None, None, :] <= query_pos[None, :, None]
        probability = jnp.where(allowed, jnp.exp(scores - sums_in.T[:, :, None]), 0.0)
        d_probs = jnp.einsum('tgd,ngd->gtn', grads_in, value_rows)
        d_scores = bf16_keep(probability * (d_probs - delta_in.T[:, :, None])).astype(jnp.float32)
        probs_b = bf16_keep(probability).astype(jnp.float32)
        d_query = jnp.einsum('gtn,ngd->tgd', d_scores, key_rows) * inv_root
        key_total = key_total + jnp.einsum('gtn,tgd->ngd', d_scores, queries) * inv_root
        value_total = value_total + jnp.einsum('gtn,tgd->ngd', probs_b, grads_in)
        return ((key_total, value_total), d_query)
    starts = jnp.arange(TOKENS // block_size, dtype=jnp.int32) * block_size
    zeros_heads = jnp.zeros((TOKENS, QH, HD), jnp.float32)
    (key_total, value_total), d_query = lax.scan(visit_block, (zeros_heads, zeros_heads), starts)
    d_key = key_total.reshape(TOKENS, KVH, group_size, HD).sum(axis=2)
    d_value = value_total.reshape(TOKENS, KVH, group_size, HD).sum(axis=2)
    return (d_query.reshape(TOKENS, QH, HD), d_key, d_value)

def reference(tokens, gain_mix, w_z, w_x, w_bc, w_dt, conv_x, conv_bc, dt_bias, a_log, d_skip, w_out, w_q, w_kv, w_o, gain_ffn, w_gate, w_up, w_down, cotangent):
    tokens_wide = tokens.astype(jnp.float32)
    scale_mix = rms_scale(tokens_wide)
    normed = bf16_keep(tokens_wide * scale_mix * gain_mix)
    z_proj = project(normed, w_z)
    x_proj = project(normed, w_x)
    bc_proj = project(normed, w_bc)
    dt_proj = project(normed, w_dt)
    ssm_gated, pull_mixer = jax.vjp(mixer_reference, z_proj, x_proj, bc_proj, dt_proj, conv_x, conv_bc, dt_bias, a_log, d_skip)
    gated = bf16_keep(ssm_gated)
    positions = jnp.arange(TOKENS, dtype=jnp.int32)
    cosine, sine = rope_tables(positions)
    q_proj = project(normed, w_q).reshape(TOKENS, QH, HD)
    kv_proj = project(normed, w_kv)
    k_proj = kv_proj[:, :KVH * HD].reshape(TOKENS, KVH, HD)
    v_val = bf16_keep(kv_proj[:, KVH * HD:].reshape(TOKENS, KVH, HD))
    q_rot = bf16_keep(rotate(q_proj, cosine, sine))
    k_rot = bf16_keep(rotate(k_proj, cosine, sine))
    attn_heads, log_sums = attention_forward(q_rot, k_rot, v_val)
    attn_out = attn_heads.reshape(TOKENS, QH * HD)
    hidden = tokens_wide + project(gated, w_out) + project(attn_out, w_o)
    scale_ffn = rms_scale(hidden)
    hnormed = bf16_keep(hidden * scale_ffn * gain_ffn)
    gate_proj = project(hnormed, w_gate)
    up_proj = project(hnormed, w_up)
    activated = bf16_keep(jax.nn.silu(gate_proj) * up_proj)
    output = (hidden + project(activated, w_down)).astype(jnp.bfloat16)
    cot_wide = cotangent.astype(jnp.float32)
    d_act = project(cotangent, w_down.T)
    sigmoid_gate = jax.nn.sigmoid(gate_proj)
    d_gate = bf16_keep(d_act * up_proj * sigmoid_gate * (1.0 + gate_proj * (1.0 - sigmoid_gate)))
    d_up = bf16_keep(d_act * gate_proj * sigmoid_gate)
    d_hnormed = project(d_gate, w_gate.T) + project(d_up, w_up.T)
    hidden_hat = hidden * scale_ffn
    weighted_ffn = d_hnormed * gain_ffn
    d_hidden = cot_wide + scale_ffn * (weighted_ffn - hidden_hat * lax.optimization_barrier(jnp.mean(weighted_ffn * hidden_hat, axis=-1, keepdims=True)))
    grad_gain_ffn = lax.optimization_barrier(jnp.sum(d_hnormed * hidden_hat, axis=0))
    d_hidden_b = bf16_keep(d_hidden)
    d_gated = project(d_hidden_b, w_out.T)
    d_attn = bf16_keep(project(d_hidden_b, w_o.T)).reshape(TOKENS, QH, HD)
    out_delta = lax.optimization_barrier(jnp.sum(d_attn.astype(jnp.float32) * attn_heads.astype(jnp.float32), axis=-1))
    d_q_rot, d_k_rot, d_value = attention_backward(q_rot, k_rot, v_val, d_attn, log_sums, out_delta)
    d_q = bf16_keep(unrotate(d_q_rot, cosine, sine).reshape(TOKENS, QH * HD))
    d_kv = bf16_keep(jnp.concatenate([unrotate(d_k_rot, cosine, sine).reshape(TOKENS, KVH * HD), d_value.reshape(TOKENS, KVH * HD)], axis=1))
    d_z, d_x, d_bc, d_dt, grad_conv_x, grad_conv_bc, grad_dt_bias, grad_a_log, grad_d_skip = pull_mixer(d_gated)
    d_z_b = bf16_keep(d_z)
    d_x_b = bf16_keep(d_x)
    d_bc_b = bf16_keep(d_bc)
    d_dt_b = bf16_keep(d_dt)
    d_normed = project(d_z_b, w_z.T) + project(d_x_b, w_x.T) + project(d_bc_b, w_bc.T) + project(d_dt_b, w_dt.T) + project(d_q, w_q.T) + project(d_kv, w_kv.T)
    tokens_hat = tokens_wide * scale_mix
    weighted_mix = d_normed * gain_mix
    grad_tokens = d_hidden + scale_mix * (weighted_mix - tokens_hat * lax.optimization_barrier(jnp.mean(weighted_mix * tokens_hat, axis=-1, keepdims=True)))
    grad_gain_mix = lax.optimization_barrier(jnp.sum(d_normed * tokens_hat, axis=0))
    return (output, grad_tokens, grad_gain_mix, project(normed.T, d_z_b), project(normed.T, d_x_b), project(normed.T, d_bc_b), project(normed.T, d_dt_b), grad_conv_x, grad_conv_bc, grad_dt_bias, grad_a_log, grad_d_skip, project(gated.T, d_hidden_b), project(normed.T, d_q), project(normed.T, d_kv), project(attn_out.T, d_hidden_b), grad_gain_ffn, project(hnormed.T, d_gate), project(hnormed.T, d_up), project(activated.T, cotangent))
```

```python
import jax
import jax.numpy as jnp
from jax import lax
from jax.sharding import PartitionSpec as P

NS = 128
CONVK = 4
QH = 8
KVH = 2
HD = 64


EPS = 1e-05
ROPE_BASE = 100000000000.0
highest = lax.Precision.HIGHEST


def passed_along(value, axis, steps):
    count = lax.axis_size(axis)
    leading, last = (max(0, -steps), min(count, count - steps))
    return lax.ppermute(value, axis, [(source, source + steps) for source in range(leading, last)])


def project(left_side, right_side):
    return jnp.dot(left_side, right_side, preferred_element_type=jnp.float32)


def rms_scale(row_values):
    return lax.rsqrt(jnp.mean(row_values * row_values, axis=-1, keepdims=True) + EPS)


def rope_tables(positions):
    frequency = ROPE_BASE ** (-(jnp.arange(HD // 2, dtype=jnp.float32) * 2.0 / HD))
    angles = positions.astype(jnp.float32)[:, None] * frequency[None, :]
    return (jnp.cos(angles), jnp.sin(angles))


def rotate(values, cosine, sine):
    half_width = values.shape[-1] // 2
    first_half = values[..., :half_width]
    second_half = values[..., half_width:]
    cos_part = cosine[:, None, :]
    sin_part = sine[:, None, :]
    return jnp.concatenate(
        [
            first_half * cos_part - second_half * sin_part,
            second_half * cos_part + first_half * sin_part,
        ],
        axis=-1,
    )


def unrotate(gradients, cosine, sine):
    half_width = gradients.shape[-1] // 2
    first_half = gradients[..., :half_width]
    second_half = gradients[..., half_width:]
    cos_part = cosine[:, None, :]
    sin_part = sine[:, None, :]
    return jnp.concatenate(
        [
            first_half * cos_part + second_half * sin_part,
            second_half * cos_part - first_half * sin_part,
        ],
        axis=-1,
    )


HALO = 16
SUM_TYPE = jnp.bfloat16
LANES = 128


def rounded_up(width):
    return -(-width // LANES) * LANES


def prepare(x_rows, bc_rows, dt_input, conv_x, conv_bc, dt_bias, a_log):
    length, head_count = dt_input.shape

    def conv_silu(padded, kernel):
        first = padded.shape[0] - length - CONVK + 1
        running = kernel[0] * padded[first : first + length]
        for offset in range(1, CONVK):
            running = running + kernel[offset] * padded[first + offset : first + offset + length]
        return jax.nn.silu(running)

    x_heads = conv_silu(x_rows, conv_x).reshape(length, head_count, -1).transpose(1, 0, 2)
    bc_conv = conv_silu(bc_rows, conv_bc)
    step_size = jax.nn.softplus(dt_input + dt_bias[None, :]).T
    log_decay = -jnp.exp(a_log)[:, None] * step_size
    ticks = jnp.arange(length, dtype=jnp.int32)
    upto = (ticks[:, None] <= ticks[None, :]).astype(jnp.float32)
    cumulative = jnp.dot(log_decay, upto, precision=highest)
    return (x_heads, bc_conv[:, :NS], bc_conv[:, NS:], step_size, cumulative)


def ssd_state(x_heads, b_mat, step_size, cumulative):
    tail_weight = jnp.exp(cumulative[:, -1:] - cumulative) * step_size
    local_state = jnp.einsum(
        "hsp,sn->hpn", x_heads * tail_weight[:, :, None], b_mat, precision=highest
    )
    return (cumulative[:, -1], local_state)


def ssd_gated(z_input, x_heads, b_mat, c_mat, step_size, cumulative, d_skip, start_state):
    head_count, length, _ = x_heads.shape
    ticks = jnp.arange(length, dtype=jnp.int32)
    causal = ticks[:, None] >= ticks[None, :]
    gap_sums = cumulative[:, :, None] - cumulative[:, None, :]
    decays = jnp.exp(jnp.where(causal[None], gap_sums, -1e30))
    intersections = lax.dot_general(c_mat, b_mat, (((1,), (1,)), ((), ())), precision=highest)
    mixing = decays * intersections[None] * step_size[:, None, :]
    inner_part = jnp.einsum("hts,hsp->htp", mixing, x_heads, precision=highest)
    carried = (
        jnp.einsum("tn,hpn->htp", c_mat, start_state, precision=highest)
        * jnp.exp(cumulative)[:, :, None]
    )
    ssm_out = inner_part + carried + d_skip[:, None, None] * x_heads
    return ssm_out.transpose(1, 0, 2).reshape(length, -1) * jax.nn.silu(z_input)


def times(left_side, right_side, left_dim, right_dim):
    return lax.dot_general(
        left_side,
        right_side,
        (((left_dim,), (right_dim,)), ((), ())),
        preferred_element_type=jnp.float32,
    )


def split_columns(packed, widths):
    pieces, at = ([], 0)
    for width in widths:
        pieces.append(packed[:, at : at + width])
        at += rounded_up(width)
    return pieces


def padded_columns(values):
    return jnp.pad(values, ((0, 0), (0, rounded_up(values.shape[1]) - values.shape[1])))


def pack_columns(pieces):
    return jnp.concatenate([padded_columns(piece) for piece in pieces], axis=1)


def seq_gather(values):
    return lax.all_gather(values, "seq", axis=0, tiled=False)


def seq_reduce(values):
    return lax.psum_scatter(values, "seq", scatter_dimension=0, tiled=False)


def grads_reduce(values):
    return lax.psum_scatter(values, "seq", scatter_dimension=0, tiled=True)


def wa_sum(values):
    return lax.psum(values, "wa")


def split_three(values):
    high = values.astype(jnp.bfloat16)
    left = values - lax.reduce_precision(values, 8, 7)
    middle = left.astype(jnp.bfloat16)
    low = (left - lax.reduce_precision(left, 8, 7)).astype(jnp.bfloat16)
    return (high, middle, low)


def per_device(
    tokens,
    gain_mix,
    w_z,
    w_x,
    w_bc,
    w_dt,
    conv_x,
    conv_bc,
    dt_bias,
    a_log,
    d_skip,
    w_out,
    w_q,
    w_kv,
    w_o,
    gain_ffn,
    w_gate,
    w_up,
    w_down,
    cotangent,
):
    rows, width = tokens.shape
    seq_count = lax.axis_size("seq")
    seq_index = lax.axis_index("seq")
    wa_index = lax.axis_index("wa")
    head_count = a_log.shape[0]
    state_rows = head_count * (w_x.shape[1] // head_count)
    before = passed_along(tokens[rows - HALO :], "seq", 1)
    weights = (w_z, w_x, w_bc, w_q, w_kv, w_dt, w_gate, w_up, w_out.T, w_o.T, w_down.T)
    widths = [w.shape[1] for w in weights]
    first_width = sum(rounded_up(w) for w in widths[:6])
    gate_width = first_width + widths[6] + widths[7]
    mixed_width = gate_width + widths[8] + widths[9]
    full = lax.all_gather(pack_columns(weights), "seq", axis=0, tiled=True)
    full_first = full[:, :first_width]
    full_ffn = full[:, first_width:gate_width]
    full_mixed = full[:, gate_width:mixed_width]
    full_down = full[:, mixed_width:]

    def normalised(values):
        wide = values.astype(jnp.float32)
        return (wide * rms_scale(wide) * gain_mix).astype(jnp.bfloat16)

    tokens_wide = tokens.astype(jnp.float32)
    scale_mix = rms_scale(tokens_wide)
    normed = (tokens_wide * scale_mix * gain_mix).astype(jnp.bfloat16)
    extended = jnp.concatenate([normalised(before), normed], axis=0)
    projected = project(extended, full_first)
    z_rows, x_rows, bc_rows, q_rows, kv_rows, dt_rows = split_columns(projected, widths[:6])
    z_proj = z_rows[HALO:]
    mixer_inputs = (x_rows, bc_rows, dt_rows[HALO:], conv_x, conv_bc, dt_bias, a_log)
    prepared, pull_prepare = jax.vjp(prepare, *mixer_inputs)
    x_heads, b_mat, c_mat, step_size, cumulative = prepared
    (log_total, local_state), pull_state = jax.vjp(
        ssd_state, x_heads, b_mat, step_size, cumulative
    )

    local_query = w_q.shape[1] // HD
    kv_head = wa_index * local_query // (QH // KVH)
    positions = seq_index * rows + jnp.arange(rows, dtype=jnp.int32)
    cosine, sine = rope_tables(positions)
    q_proj = q_rows[HALO:].reshape(rows, local_query, HD)
    kv_proj = kv_rows[HALO:]
    k_proj = lax.dynamic_slice_in_dim(kv_proj, kv_head * HD, HD, 1)
    v_proj = lax.dynamic_slice_in_dim(kv_proj, KVH * HD + kv_head * HD, HD, 1)
    q_rot = rotate(q_proj, cosine, sine).astype(jnp.bfloat16).transpose(1, 0, 2)
    k_rot = rotate(k_proj[:, None, :], cosine, sine)[:, 0, :]
    total_rows = jnp.pad(
        jnp.stack(split_three(log_total)), ((0, HALO - 3), (0, LANES - head_count))
    )
    sent = jnp.concatenate(
        [
            jnp.concatenate([k_rot, v_proj], axis=1).astype(jnp.bfloat16),
            local_state.reshape(state_rows, NS).astype(jnp.bfloat16),
            total_rows,
        ],
        axis=0,
    )
    arrived = seq_gather(sent)
    key_all = arrived[:, :rows, :HD].reshape(seq_count * rows, HD)
    value_all = arrived[:, :rows, HD:].reshape(seq_count * rows, HD)
    states = arrived[:, rows : rows + state_rows].astype(jnp.float32)
    totals = jnp.sum(
        arrived[:, rows + state_rows : rows + state_rows + 3, :head_count].astype(jnp.float32),
        axis=1,
    )
    blocks = jnp.arange(seq_count, dtype=jnp.int32)
    low_end = jnp.minimum(blocks, seq_index)
    high_end = jnp.maximum(blocks, seq_index)
    between = (blocks[None, :] > low_end[:, None]) & (blocks[None, :] < high_end[:, None])
    path_decay = jnp.exp(jnp.sum(jnp.where(between[:, :, None], totals[None], 0.0), axis=1))
    earlier = jnp.where((blocks < seq_index)[:, None], path_decay, 0.0)
    later = jnp.where((blocks < seq_index)[:, None], path_decay, 0.0)
    shape_all = (seq_count, head_count, state_rows // head_count, NS)
    start_state = jnp.sum(earlier[:, :, None, None] * states.reshape(shape_all), axis=0)
    ssm_gated, pull_output = jax.vjp(
        ssd_gated, z_proj, x_heads, b_mat, c_mat, step_size, cumulative, d_skip, start_state
    )
    gated = ssm_gated.astype(jnp.bfloat16)

    key_pos = jnp.arange(seq_count * rows, dtype=jnp.int32)
    allowed = (key_pos[None, :] <= positions[:, None])[None]

    def per_head(left_side, right_side, left_dim, right_dim):
        return jnp.stack(
            [times(left_side[g], right_side, left_dim, right_dim) for g in range(local_query)]
        )

    scores = jnp.where(allowed, per_head(q_rot, key_all, 1, 1) * HD ** (-0.5), -1e30)
    row_max = jnp.max(scores, axis=-1, keepdims=True)
    attn_weights = jnp.exp(scores - row_max)
    row_sum = jnp.sum(attn_weights, axis=-1, keepdims=True)
    weighted_sum = per_head(attn_weights.astype(jnp.bfloat16), value_all, 1, 0)
    attn_heads = (weighted_sum / row_sum).astype(jnp.bfloat16)
    log_sums = row_max + jnp.log(row_sum)
    attn_out = attn_heads.transpose(1, 0, 2).reshape(rows, local_query * HD)
    mixed = jnp.concatenate([gated, attn_out], axis=1)
    hidden = tokens_wide + wa_sum(times(mixed, full_mixed, 1, 1))
    scale_ffn = rms_scale(hidden)
    hnormed = (hidden * scale_ffn * gain_ffn).astype(jnp.bfloat16)
    ffn_width = widths[6]
    ffn_proj = project(hnormed, full_ffn)
    gate_proj = ffn_proj[:, :ffn_width]
    up_proj = ffn_proj[:, ffn_width:]
    activated = (jax.nn.silu(gate_proj) * up_proj).astype(jnp.bfloat16)
    ffn_part = times(activated, full_down, 1, 1)
    cot_wide = cotangent.astype(jnp.float32)
    d_act = project(cotangent, full_down)
    sigmoid_gate = jax.nn.sigmoid(gate_proj)
    d_gate = d_act * up_proj * sigmoid_gate * (1.0 + gate_proj * (1.0 - sigmoid_gate))
    d_up = d_act * gate_proj * sigmoid_gate
    d_ffn = jnp.concatenate([d_gate.astype(jnp.bfloat16), d_up.astype(jnp.bfloat16)], axis=1)
    d_hnormed = wa_sum(times(d_ffn, full_ffn, 1, 1))
    hidden_hat = hidden * scale_ffn
    weighted_ffn = d_hnormed * gain_ffn
    d_hidden = cot_wide + scale_ffn * (
        weighted_ffn - hidden_hat * jnp.mean(weighted_ffn * hidden_hat, axis=-1, keepdims=True)
    )
    grad_gain_ffn = jnp.sum(d_hnormed * hidden_hat, axis=0)
    d_hidden_b = d_hidden.astype(jnp.bfloat16)
    d_mixed = project(d_hidden_b, full_mixed)
    inner_width = widths[8]
    d_gated = d_mixed[:, :inner_width]
    d_attn_heads = (
        d_mixed[:, inner_width:]
        .astype(jnp.bfloat16)
        .reshape(rows, local_query, HD)
        .transpose(1, 0, 2)
    )
    out_grads = pull_output(d_gated)
    direct = out_grads[7]
    out_delta = jnp.sum(
        d_attn_heads.astype(jnp.float32) * attn_heads.astype(jnp.float32), axis=-1, keepdims=True
    )
    probability = jnp.exp(scores - log_sums)
    d_probs = per_head(d_attn_heads, value_all, 1, 1)
    d_scores = (probability * (d_probs - out_delta)).astype(jnp.bfloat16)
    flat_rows = (local_query * rows, -1)
    d_key = times(d_scores.reshape(flat_rows), q_rot.reshape(flat_rows), 0, 0) * HD ** (-0.5)
    d_value = times(
        probability.astype(jnp.bfloat16).reshape(flat_rows), d_attn_heads.reshape(flat_rows), 0, 0
    )
    key_parts = jnp.concatenate([d_key, d_value], axis=1).reshape(seq_count, rows, 2 * HD)
    state_parts = (later[:, :, None, None] * direct[None]).reshape(seq_count, state_rows, NS)
    own_parts = seq_reduce(
        jnp.concatenate([key_parts, state_parts], axis=1).astype(SUM_TYPE)
    ).astype(jnp.float32)
    d_q_rot = per_head(d_scores, key_all, 1, 0) * HD ** (-0.5)
    d_q = unrotate(d_q_rot.transpose(1, 0, 2), cosine, sine).reshape(rows, -1).astype(jnp.bfloat16)
    d_key_own = unrotate(own_parts[:rows, None, :HD], cosine, sine)[:, 0, :]
    d_value_own = own_parts[:rows, HD:]
    d_end = own_parts[rows:].reshape(direct.shape)
    d_total = jnp.exp(log_total) * jnp.sum(d_end * start_state, axis=(1, 2))
    state_grads = pull_state((d_total, d_end))
    merged = (
        out_grads[1] + state_grads[0],
        out_grads[2] + state_grads[1],
        out_grads[3],
        out_grads[4] + state_grads[2],
        out_grads[5] + state_grads[3],
    )
    (
        d_x_rows,
        d_bc_rows,
        d_dt_in,
        grad_conv_x,
        grad_conv_bc,
        grad_dt_bias,
        grad_a_log,
    ) = pull_prepare(merged)
    x_width = widths[1]
    edge_back = passed_along(
        jnp.concatenate([d_x_rows[:HALO], d_bc_rows[:HALO]], axis=1), "seq", -1
    )
    d_x_in = d_x_rows[HALO:].at[rows - HALO :].add(edge_back[:, :x_width])
    d_bc_in = d_bc_rows[HALO:].at[rows - HALO :].add(edge_back[:, x_width:])
    d_z_b = out_grads[0].astype(jnp.bfloat16)
    d_x_b = d_x_in.astype(jnp.bfloat16)
    d_dt_b = d_dt_in.astype(jnp.bfloat16)
    head_pick = (jnp.arange(KVH, dtype=jnp.int32) == kv_head).astype(jnp.float32)
    d_kv_part = jnp.concatenate(
        [head_pick[k] * part for part in (d_key_own, d_value_own) for k in range(KVH)], axis=1
    )
    full_z, full_x, full_bc, full_q, full_kv, full_dt = split_columns(full_first, widths[:6])
    d_normed_part = (
        times(jnp.concatenate([d_z_b, d_x_b], axis=1), full[:, : widths[0] + x_width], 1, 1)
        + times(d_dt_b, full_dt, 1, 1)
        + times(d_q, full_q, 1, 1)
    )
    shared = jnp.concatenate([d_normed_part, d_bc_in, d_kv_part], axis=1)
    conv_rows = jnp.pad(
        grad_conv_bc, ((0, 8 - CONVK), (0, shared.shape[1] - grad_conv_bc.shape[1]))
    )
    shared = wa_sum(jnp.concatenate([shared, conv_rows], axis=0))
    d_normed_sum = shared[:rows, :width]
    d_bckv_b = shared[:rows, width:].astype(jnp.bfloat16)
    grad_conv_bc = shared[rows : rows + CONVK, : grad_conv_bc.shape[1]]
    d_bc_b = d_bckv_b[:, : widths[2]]
    d_kv_b = d_bckv_b[:, widths[2] :]
    d_normed = d_normed_sum + times(d_bc_b, full_bc, 1, 1) + times(d_kv_b, full_kv, 1, 1)
    tokens_hat = tokens_wide * scale_mix
    weighted_mix = d_normed * gain_mix
    grad_tokens = d_hidden + scale_mix * (
        weighted_mix - tokens_hat * jnp.mean(weighted_mix * tokens_hat, axis=-1, keepdims=True)
    )
    grad_gain_mix = jnp.sum(d_normed * tokens_hat, axis=0)
    ffn_own = lax.psum_scatter(ffn_part, "wa", scatter_dimension=1, tiled=True)
    own_width = ffn_own.shape[1]
    hidden_own = lax.dynamic_slice_in_dim(hidden, wa_index * own_width, own_width, 1)
    output = (hidden_own + ffn_own).astype(jnp.bfloat16)
    d_first = pack_columns([d_z_b, d_x_b, d_bc_b, d_q, d_kv_b, d_dt_b])
    parts = jnp.concatenate(
        [
            times(normed, d_first, 0, 0).astype(SUM_TYPE),
            times(hnormed, d_ffn, 0, 0).astype(SUM_TYPE),
            times(d_hidden_b, mixed, 0, 0).astype(SUM_TYPE),
            times(cotangent, activated, 0, 0).astype(SUM_TYPE),
        ],
        axis=1,
    )
    own = grads_reduce(parts).astype(jnp.float32)
    grads = split_columns(own, widths)
    small = (
        grad_gain_mix,
        grad_gain_ffn,
        grad_conv_x.reshape(-1),
        grad_conv_bc.reshape(-1),
        grad_dt_bias,
        grad_a_log,
        out_grads[6],
    )
    small_sum = lax.psum(jnp.concatenate(small), "seq")
    sums, at = ([], 0)
    for piece in small:
        sums.append(small_sum[at : at + piece.shape[0]])
        at += piece.shape[0]
    return (
        output,
        grad_tokens,
        sums[0],
        grads[0],
        grads[1],
        grads[2],
        grads[5],
        sums[2].reshape(conv_x.shape),
        sums[3].reshape(conv_bc.shape),
        sums[4],
        sums[5],
        sums[6],
        grads[8].T,
        grads[3],
        grads[4],
        grads[9].T,
        sums[1],
        grads[6],
        grads[7],
        grads[10].T,
    )


def solution(mesh):
    placed = (
        P("seq", None),
        P(),
        P("seq", "wa"),
        P("seq", "wa"),
        P("seq", None),
        P("seq", "wa"),
        P(None, "wa"),
        P(),
        P("wa"),
        P("wa"),
        P("wa"),
        P("wa", "seq"),
        P("seq", "wa"),
        P("seq", None),
        P("wa", "seq"),
        P(),
        P("seq", "wa"),
        P("seq", "wa"),
        P("wa", "seq"),
        P("seq", None),
    )
    return jax.shard_map(
        per_device,
        mesh=mesh,
        in_specs=placed,
        out_specs=(
            P("seq", "wa"),
            P("seq", None),
            P(),
            P("seq", "wa"),
            P("seq", "wa"),
            P("seq", None),
            P("seq", "wa"),
            P(None, "wa"),
            P(),
            P("wa"),
            P("wa"),
            P("wa"),
            P("wa", "seq"),
            P("seq", "wa"),
            P("seq", None),
            P("wa", "seq"),
            P(),
            P("seq", "wa"),
            P("seq", "wa"),
            P("wa", "seq"),
        ),
        check_vma=False,
    )
```
